32 devices in a mesh: segment: 2 (over core), gx: 2 (over x), gy: 4 (over z), gz: 2 (over y).
Axes of the slice: x: 2, y: 2, z: 4, core: 2. Of those that a mesh axis runs over, the one named last changes fastest.
Arguments:
- features: bfloat16 [2, 16, 8, 128, 256], P(None, None, 'gx', 'gy', 'gz'), may hold values from -6 to 6
- weights: bfloat16 [2, 2, 16, 16, 3, 3, 3], P('segment'), may hold values from -0.4375 to 0.4375
- biases: bfloat16 [2, 2, 16], P('segment'), may hold values from -3 to 3
Outputs:
- section_out: bfloat16 [2, 2, 16, 8, 128, 256], P('segment', None, None, 'gx', 'gy', 'gz')
The draws below stay inside these ranges and needn't reach their ends.
All inputs are finite; a program needn't handle non-finite values.
Results may differ from the reference program's by a relative error of at most 0.0054.
Values may be sent and summed in bfloat16 or wider, within the bound.
No kernel may reach another device: no remote copies, remote signals or barrier semaphores. Data moves between devices by JAX's collectives and lax.ppermute only.
A program may use at most 64 MiB of HBM per device.

```python
import jax
import jax.numpy as jnp
from jax import lax

C = 16
MICRO = 2
NX = 8
NY = 128
NZ = 256


def block_scale(key, dims, cuts, least, top_value):
    def one(position, shards_of):
        heights = jax.random.uniform(jax.random.fold_in(jax.random.fold_in(key, 6), position), (shards_of,), jnp.float32, least / len(cuts), top_value / len(cuts))
        return jnp.repeat(jnp.exp(heights), dims[position] // shards_of).reshape((-1,) + (1,) * (len(dims) - position - 1))

    loudness = one(*cuts[0])
    for cut in cuts[1:]:
        loudness = loudness * one(*cut)
    return loudness


def scatter_about(stream_key, shape, scale, limit, cuts=(), held_as=jnp.bfloat16):
    result = scale * jax.random.normal(stream_key, shape, jnp.float32)
    if cuts:
        result = result * block_scale(stream_key, shape, cuts, -0.22, 0.18)
    return jnp.clip(result, -limit, limit).astype(held_as)


def setup_inputs(seed: int = 0) -> dict:
    key_of = jax.random.split(jax.random.key(seed), 4)
    features = scatter_about(key_of[0], (MICRO, C, NX, NY, NZ), 1.0, 6.0, ((2, 2), (3, 4), (4, 2)))
    weights = scatter_about(key_of[1], (2, 2, C, C, 3, 3, 3), (27 * C // 2) ** -0.5, 0.4375, ((0, 2),))
    biases = scatter_about(key_of[2], (2, 2, C), 0.5, 3.0, ((0, 2),))
    return dict(features=features, weights=weights, biases=biases)


def convolve(field, kernel, offset):
    linear = lax.conv_general_dilated(field[None], kernel, (1, 1, 1), ((1, 1), (1, 1), (1, 1)), dimension_numbers=("NCDHW", "OIDHW", "NCDHW"), preferred_element_type=jnp.float32)[0]
    summed = linear + offset.astype(jnp.float32)[:, None, None, None]
    return jnp.where(summed > 0, summed, 0.2 * summed).astype(jnp.bfloat16)


def reference(features, weights, biases):
    first_list = []
    second_list = []
    for batch_index in range(MICRO):
        hidden = features[batch_index]
        hidden = convolve(convolve(hidden, weights[0, 0], biases[0, 0]), weights[0, 1], biases[0, 1])
        first_list.append(hidden)
        hidden = convolve(convolve(hidden, weights[1, 0], biases[1, 0]), weights[1, 1], biases[1, 1])
        second_list.append(hidden)
    return jnp.stack([jnp.stack(first_list), jnp.stack(second_list)])
```

```python
import functools

import jax
import jax.numpy as jnp
from jax import lax
from jax.experimental import pallas as pl
from jax.experimental.pallas import tpu as pltpu
from jax.sharding import PartitionSpec as P

WIDE = 4
SEG = 16
BF = jnp.bfloat16
F32 = jnp.float32


def swap_pairs(size):
    return [(i, i ^ 1) for i in range(size) if i ^ 1 < size]


def shifted_pairs(size):
    return [(i, j) for i in range(1, size - 1, 2) for j in [i + 1]] + [
        (i + 1, i) for i in range(1, size - 1, 2)
    ]


def transposer():
    row = lax.broadcasted_iota(jnp.int32, (256, 256), 0)
    col = lax.broadcasted_iota(jnp.int32, (256, 256), 1)
    hit = ((row >> 4) == (col & 15)) & ((row & 15) == (col >> 4))
    return jnp.where(hit, 1.0, 0.0).astype(BF)


def lane_mask(test):
    lane = lax.broadcasted_iota(jnp.int32, (16, 128), 1)
    return jnp.where(test(lane), 1.0, 0.0).astype(BF)


def swap_rows(turn, blocks):
    wide = jnp.concatenate(blocks, 1) if len(blocks) > 1 else blocks[0]
    turned = jnp.dot(turn, wide, preferred_element_type=F32).astype(BF)
    return [turned[:, k * 128 : (k + 1) * 128].reshape(16, 16, 128) for k in range(len(blocks))]


def to_tiles(turn, ref, x, store):
    rows = ref.shape[2]
    starts = list(range(0, rows, 16))
    for k in range(0, len(starts), 2):
        some = starts[k : k + 2]
        for y0, block in zip(some, swap_rows(turn, [ref[:, x, y0 : y0 + 16, :].reshape(256, 128) for y0 in some])):
            store(y0, block)


def pack_kernel(x_ref, tile_ref, z_ref, a_ref, b_ref):
    depth, rows = tile_ref.shape[0], tile_ref.shape[1]
    right = lax.axis_index("gz") == 0
    even = lax.rem(lax.axis_index("gy"), 2) == 0
    turn = transposer()
    turned_by = jnp.where(right, WIDE, 0)
    for x in range(depth):

        def store(y0, block):
            tile_ref[x, y0 : y0 + 16] = block

        to_tiles(turn, x_ref, x, store)
    for x in range(depth):
        parts = [jnp.zeros((16, 128), BF) for _ in range(4)]
        for y in range(rows):
            mask = lane_mask(lambda lane: (lane >> 2) == y)
            moved = pltpu.roll(tile_ref[x, y], 4 * y, 1) if y else tile_ref[x, y]
            early = lane_mask(lambda lane: (((lane + turned_by) & 127) >> 2) == y)
            parts[y % 4] = parts[y % 4] + moved * early
        total = (parts[0] + parts[1]) + (parts[2] + parts[3])
        z_ref[x] = pltpu.roll(total, turned_by, 1)
    first = jnp.where(even, rows - WIDE, 0)
    second = jnp.where(even, 0, rows - WIDE)
    for x in range(depth):
        a_ref[x * WIDE : (x + 1) * WIDE] = tile_ref[x, pl.ds(first, WIDE)]
        b_ref[x * WIDE : (x + 1) * WIDE] = tile_ref[x, pl.ds(second, WIDE)]


def weight_kernel(flip_x, w_ref, b_ref, t_ref):
    layers = w_ref.shape[0]
    zero = jnp.zeros((16, 16), BF)
    flipped = lax.axis_index("gx") == 1 if flip_x else None
    row = lax.broadcasted_iota(jnp.int32, (16, 16), 0)
    col = lax.broadcasted_iota(jnp.int32, (16, 16), 1)
    for layer in range(layers):
        for dz in range(3):
            for xo in range(2):
                for yo in range(2):
                    pieces = []
                    for xi in range(4):
                        for yi in range(4):
                            dx, dy = xi - xo, yi - yo
                            if 0 <= dx < 3 and 0 <= dy < 3:
                                at = jnp.where(flipped, 2 - dx, dx) if flip_x else dx
                                pieces.append(w_ref[layer, at, dy, dz])
                            else:
                                pieces.append(zero)
                    at_row = ((dz * 2 + xo) * 2 + yo) * 16
                    t_ref[layer, at_row : at_row + 16] = jnp.concatenate(pieces, 1)
        spread = jnp.broadcast_to(b_ref[layer : layer + 1, :].astype(F32), (16, 16))
        column = jnp.sum(jnp.where(row == col, spread, 0.0), axis=1, keepdims=True)
        t_ref[layer, 192:208] = jnp.broadcast_to(column, (16, 256)).astype(BF)


def main_kernel(two_sided, counts, own_ref, halo_ref, *rest):
    sides = 2 if two_sided else 1
    raws, halos = rest[:sides], rest[sides : 2 * sides]
    t_ref, keep_ref, send_ref = rest[2 * sides : 2 * sides + 3]
    va, vb, sa, sb, bias_ref, out_ref, sems = rest[2 * sides + 3 :]
    depth, rows = own_ref.shape[0], own_ref.shape[1]
    ext_rows = rows + 2 * WIDE
    per = sa.shape[1] - 2
    segments = 128 // SEG
    blk = depth * WIDE + depth
    section = lax.axis_index("segment")
    gx, gy = lax.axis_index("gx"), lax.axis_index("gy")
    right = lax.axis_index("gz") == 0
    even = lax.rem(gy, 2) == 0
    top_ok = jnp.where(gy == 0, 0.0, 1.0).astype(F32)
    low_ok = jnp.where(gy == counts["gy"] - 1, 0.0, 1.0).astype(F32)
    prev_at = jnp.where(even, blk, 0)
    next_at = jnp.where(even, 0, blk)
    turn = transposer()
    zero_tile = jnp.zeros((16, 128), BF)

    def flip(i):
        return i if two_sided else jnp.where(gx == 1, depth - 1 - i, i)

    slabs = [(0, flip(i)) for i in range(depth)]
    if two_sided:
        slabs = [(1, depth - WIDE + i) for i in range(WIDE)] + slabs + [(2, i) for i in range(WIDE)]
        own_at = WIDE
    else:
        slabs = slabs + [(1, flip(i)) for i in range(WIDE)]
        own_at = 0
    ext = len(slabs)

    for v, s in ((va, sa), (vb, sb)):
        for x in (0, ext + 1):
            v[x] = jnp.zeros(v.shape[1:], BF)
            s[x] = jnp.zeros(s.shape[1:], BF)
        for x in range(ext + 2):
            v[x, 0] = zero_tile
            v[x, ext_rows + 1] = zero_tile

    ahead = jnp.where(right, 3 * WIDE, 0)
    own_masks = [
        lane_mask(
            lambda lane: ((((lane + ahead) & 127) >> 4) == j) & (((lane + ahead) & 15) < 3 * WIDE)
        )
        for j in range(segments)
    ]
    halo_masks = [lane_mask(lambda lane: ((lane >> 4) == j) & ((lane & 15) < WIDE)) for j in range(segments)]
    own_turn = jnp.where(right, 3 * WIDE, WIDE)
    halo_turn = jnp.where(right, 3 * WIDE, 0)

    for p, (source, i) in enumerate(slabs):
        h = halo_ref if source == 0 else halos[source - 1]
        if source == 0:
            va[p + 1, 1 + WIDE : 1 + WIDE + rows] = own_ref[i]
        else:

            def store(y0, block):
                va[p + 1, 1 + WIDE + y0 : 1 + WIDE + y0 + 16] = block

            to_tiles(turn, raws[source - 1], i, store)
        va[p + 1, 1 : 1 + WIDE] = h[pl.ds(prev_at + i * WIDE, WIDE)]
        va[p + 1, 1 + WIDE + rows : 1 + 2 * WIDE + rows] = h[pl.ds(next_at + i * WIDE, WIDE)]
        edge_prev = h[prev_at + depth * WIDE + i]
        edge_own = h[2 * blk + i]
        edge_next = h[next_at + depth * WIDE + i]
        for yo in range(per):
            own_sum, halo_sum = zero_tile, zero_tile
            for j in range(segments):
                r = per * j + yo
                if r >= ext_rows:
                    continue
                row = va[p + 1, 1 + r]
                own_sum = own_sum + (pltpu.roll(row, SEG * j, 1) if j else row) * own_masks[j]
                if r < WIDE:
                    edge, lane = edge_prev, WIDE * (rows - WIDE + r)
                elif r < WIDE + rows:
                    edge, lane = edge_own, WIDE * (r - WIDE)
                else:
                    edge, lane = edge_next, WIDE * (r - WIDE - rows)
                by = (SEG * j - lane) % 128
                halo_sum = halo_sum + (pltpu.roll(edge, by, 1) if by else edge) * halo_masks[j]
            sa[p + 1, 1 + yo] = pltpu.roll(own_sum, own_turn, 1) + pltpu.roll(halo_sum, halo_turn, 1)
        sa[p + 1, 0] = pltpu.roll(sa[p + 1, per], SEG, 1)
        sa[p + 1, per + 1] = pltpu.roll(sa[p + 1, 1], 128 - SEG, 1)

    for layer in range(4):
        one = t_ref[layer, 192:208, :128].astype(F32)
        for k in range(4):
            bias_ref[layer, 16 * k : 16 * (k + 1)] = one

    wide_lane = lax.broadcasted_iota(jnp.int32, (64, 128), 1)
    not_first = jnp.where(wide_lane == 0, 0.0, 1.0)
    not_last = jnp.where(wide_lane == 127, 0.0, 1.0)
    strip_lane = lax.broadcasted_iota(jnp.int32, (16, 128), 1) >> 4

    def strip_ok(yo):
        r = strip_lane * per + yo
        return jnp.where(r < WIDE, top_ok, jnp.where(r >= WIDE + rows, low_ok, 1.0))

    def run_layer(layer, src, dst, ssrc, sdst, x0, groups, r0, row_groups):
        last = layer == 3

        def body(g, carry):
            at = x0 + 2 * g
            items = [(src, r0 + 2 * k, False) for k in range(row_groups)]
            items += [(ssrc, 2 * k, True) for k in range(per // 2)]
            half = len(items) // 2
            order = [[items[k], items[half + k]] for k in range(half)] + [[t] for t in items[2 * half :]]
            for pair in order:
                columns = [
                    jnp.concatenate([ref[at + xi, r : r + 4].reshape(64, 128) for xi in range(4)], 0)
                    for ref, r, _ in pair
                ]
                wide = jnp.concatenate(columns, 1) if len(columns) > 1 else columns[0]
                got = jnp.dot(t_ref[layer, :192], wide, preferred_element_type=F32)
                for k, (_, r, strip) in enumerate(pair):
                    part = got[:, 128 * k : 128 * (k + 1)]
                    a = part[64:128] + pltpu.roll(part[:64], 1, 1) * not_first
                    a = a + pltpu.roll(part[128:], 127, 1) * not_last
                    a = a + bias_ref[layer]
                    a = jnp.maximum(a, 0.2 * a)
                    for xo in range(2):
                        for yo in range(2):
                            one = a[(2 * xo + yo) * 16 : (2 * xo + yo + 1) * 16]
                            if not last:
                                if strip:
                                    one = one * strip_ok(r + yo)
                                elif r + yo < WIDE:
                                    one = one * top_ok
                                elif r + yo >= WIDE + rows:
                                    one = one * low_ok
                                if two_sided:
                                    place = at + xo
                                    outside = ((place < WIDE) & (gx == 0)) | (
                                        (place >= WIDE + depth) & (gx == counts["gx"] - 1)
                                    )
                                    one = one * jnp.where(outside, 0.0, 1.0)
                            one = one.astype(BF)
                            if strip:
                                sdst[at + xo + 1, r + yo + 1] = one
                                if r + yo == 0:
                                    sdst[at + xo + 1, per + 1] = pltpu.roll(one, 128 - SEG, 1)
                                if r + yo == per - 1:
                                    sdst[at + xo + 1, 0] = pltpu.roll(one, SEG, 1)
                            else:
                                dst[at + xo + 1, r + yo + 1] = one
            return carry

        lax.fori_loop(0, groups, body, 0)

    edge_turn = jnp.where(right, 0, 2 * WIDE)
    edge_ahead = jnp.where(right, WIDE, 0)
    edge_mask = lane_mask(lambda lane: ((lane + edge_ahead) & 127) < WIDE)
    inner_mask = lane_mask(lambda lane: ((lane + edge_ahead) & 127) >= WIDE)

    def copies(part):
        return (
            pltpu.make_async_copy(out_ref.at[part], keep_ref.at[section], sems.at[part]),
            pltpu.make_async_copy(out_ref.at[part], send_ref, sems.at[part]),
        )

    def emit(part, v, s):
        for i in range(depth):
            p = own_at + i
            to = flip(i)
            starts = list(range(0, rows, 16))
            for k in range(0, len(starts), 2):
                some = starts[k : k + 2]
                blocks = []
                for y0 in some:
                    tiles = []
                    for y in range(y0, y0 + 16):
                        r = y + WIDE
                        j, yo = r // per, r % per
                        by = (128 - 3 * WIDE - SEG * j) % 128
                        edge = pltpu.roll(s[p + 1, yo + 1], by + edge_turn, 1)
                        tiles.append(v[p + 1, r + 1] * inner_mask + edge * edge_mask)
                    blocks.append(jnp.concatenate(tiles, 0))
                for y0, block in zip(some, swap_rows(turn, blocks)):
                    out_ref[part, :, to, y0 : y0 + 16] = block
        keep, send = copies(part)

        @pl.when(section == part)
        def _():
            keep.start()

        @pl.when(section != part)
        def _():
            send.start()

    half_rows = ext_rows // 2
    spans = []
    for layer in range(1, 5):
        if two_sided:
            spans.append((layer, (ext - 2 * layer) // 2))
        else:
            spans.append((0, (depth + WIDE - layer + 1) // 2))
    run_layer(0, va, vb, sa, sb, *spans[0], 0, half_rows)
    run_layer(1, vb, va, sb, sa, *spans[1], 2, half_rows - 2)
    emit(0, va, sa)
    run_layer(2, va, vb, sa, sb, *spans[2], 2, half_rows - 2)
    run_layer(3, vb, va, sb, sa, *spans[3], WIDE, rows // 2)
    emit(1, va, sa)
    for part in range(2):
        keep, send = copies(part)

        @pl.when(section == part)
        def _():
            keep.wait()

        @pl.when(section != part)
        def _():
            send.wait()


VMEM = pl.BlockSpec(memory_space=pltpu.VMEM)
ANY = pl.BlockSpec(memory_space=pl.ANY)


def shards(counts, features, weights, biases):
    gx, gy, gz = (counts[a] for a in ("gx", "gy", "gz"))
    two_sided = gx != 2
    section = lax.axis_index("segment")
    micro, chans, depth, rows, lanes = features.shape
    mine = lax.dynamic_index_in_dim(features, section, 0, keepdims=False)

    def along_x(low, high):
        if not two_sided:
            return [lax.ppermute(low, "gx", swap_pairs(2))]
        up = [(i, i + 1) for i in range(gx - 1)]
        return [lax.ppermute(high, "gx", up), lax.ppermute(low, "gx", [(j, i) for i, j in up])]

    raws = along_x(mine, mine)
    tiles, edge_z, edge_a, edge_b = pl.pallas_call(
        pack_kernel,
        out_shape=(
            jax.ShapeDtypeStruct((depth, rows, chans, lanes), BF),
            jax.ShapeDtypeStruct((depth, chans, lanes), BF),
            jax.ShapeDtypeStruct((depth * WIDE, chans, lanes), BF),
            jax.ShapeDtypeStruct((depth * WIDE, chans, lanes), BF),
        ),
        in_specs=[VMEM],
        out_specs=(VMEM,) * 4,
        name="pack",
        cost_estimate=pl.CostEstimate(flops=4_000_000, bytes_accessed=2_000_000, transcendentals=0),
    )(mine)
    from_z = lax.ppermute(edge_z, "gz", swap_pairs(gz))
    from_a = lax.ppermute(jnp.concatenate([edge_a, from_z]), "gy", swap_pairs(gy))
    from_b = lax.ppermute(jnp.concatenate([edge_b, from_z]), "gy", shifted_pairs(gy))
    halo = jnp.concatenate([from_a, from_b, from_z])
    halos = along_x(halo, halo)

    table = pl.pallas_call(
        functools.partial(weight_kernel, not two_sided),
        out_shape=jax.ShapeDtypeStruct((2, 208, 256), BF),
        in_specs=[VMEM] * 2,
        out_specs=VMEM,
        name="weights",
        cost_estimate=pl.CostEstimate(flops=1_000_000, bytes_accessed=400_000, transcendentals=0),
    )(jnp.transpose(weights[0], (0, 3, 4, 5, 1, 2)), biases[0])
    other = lax.ppermute(table, "segment", swap_pairs(2))
    pair = jnp.stack([table, other])
    tables = jnp.where(section == 0, pair, pair[::-1]).reshape(4, 208, 256)

    ext = depth + (2 * WIDE if two_sided else WIDE)
    ext_rows = rows + 2 * WIDE
    per = -(-ext_rows * SEG // 128)
    per += per % 2
    keep, send = pl.pallas_call(
        functools.partial(main_kernel, two_sided, counts),
        out_shape=(
            jax.ShapeDtypeStruct((micro, chans, depth, rows, lanes), BF),
            jax.ShapeDtypeStruct((chans, depth, rows, lanes), BF),
        ),
        in_specs=[VMEM] * (3 + 2 * len(raws)),
        out_specs=(ANY, ANY),
        scratch_shapes=[
            pltpu.VMEM((ext + 2, ext_rows + 2, chans, lanes), BF),
            pltpu.VMEM((ext + 2, ext_rows + 2, chans, lanes), BF),
            pltpu.VMEM((ext + 2, per + 2, chans, lanes), BF),
            pltpu.VMEM((ext + 2, per + 2, chans, lanes), BF),
            pltpu.VMEM((4, 64, 128), F32),
            pltpu.VMEM((2, chans, depth, rows, lanes), BF),
            pltpu.SemaphoreType.DMA((2,)),
        ],
        name="layers",
        cost_estimate=pl.CostEstimate(flops=4_000_000_000, bytes_accessed=4_000_000, transcendentals=0),
    )(tiles, halo, *raws, *halos, tables)
    got = lax.ppermute(send, "segment", swap_pairs(2))
    return lax.dynamic_update_index_in_dim(keep, got, 1 - section, 0)[None]


def solution(mesh):
    placed = (
        P(None, None, "gx", "gy", "gz"),
        P("segment", None, None, None, None, None, None),
        P("segment", None, None),
    )
    return jax.shard_map(
        functools.partial(shards, dict(mesh.shape)),
        mesh=mesh,
        in_specs=placed,
        out_specs=P("segment", None, None, "gx", "gy", "gz"),
        check_vma=False,
    )
```

```python
import functools

import jax
import jax.numpy as jnp
from jax import lax
from jax.experimental import pallas as pl
from jax.experimental.pallas import tpu as pltpu
from jax.sharding import PartitionSpec as P


WIDE = 4
SEG = 16
BF = jnp.bfloat16
F32 = jnp.float32


def swap_pairs(size):
    return [(i, i ^ 1) for i in range(size) if i ^ 1 < size]


def shifted_pairs(size):
    return [(i, j) for i in range(1, size - 1, 2) for j in [i + 1]] + [
        (i + 1, i) for i in range(1, size - 1, 2)
    ]


def transposer():
    row = lax.broadcasted_iota(jnp.int32, (256, 256), 0)
    col = lax.broadcasted_iota(jnp.int32, (256, 256), 1)
    hit = ((row >> 4) == (col & 15)) & ((row & 15) == (col >> 4))
    return jnp.where(hit, 1.0, 0.0).astype(BF)


def lane_mask(test):
    lane = lax.broadcasted_iota(jnp.int32, (16, 128), 1)
    return jnp.where(test(lane), 1.0, 0.0).astype(BF)


def swap_rows(turn, blocks):
    wide = jnp.concatenate(blocks, 1) if len(blocks) > 1 else blocks[0]
    turned = jnp.dot(turn, wide, preferred_element_type=F32).astype(BF)
    return [turned[:, k * 128 : (k + 1) * 128].reshape(16, 16, 128) for k in range(len(blocks))]


def to_tiles(turn, ref, x, store):
    rows = ref.shape[2]
    starts = list(range(0, rows, 16))
    for k in range(0, len(starts), 2):
        some = starts[k : k + 2]
        for y0, block in zip(some, swap_rows(turn, [ref[:, x, y0 : y0 + 16, :].reshape(256, 128) for y0 in some])):
            store(y0, block)


def tile_kernel(x_hbm, tile_ref, x_ref, sems):
    depth = tile_ref.shape[0]
    section = lax.axis_index("segment")
    copies = [
        pltpu.make_async_copy(x_hbm.at[section, :, x], x_ref.at[:, x], sems.at[x]) for x in range(depth)
    ]
    for copy in copies:
        copy.start()
    turn = transposer()
    for x in range(depth):
        copies[x].wait()

        def store(y0, block):
            tile_ref[x, y0 : y0 + 16] = block

        to_tiles(turn, x_ref, x, store)


def pack_kernel(tile_ref, z_ref, a_ref, b_ref):
    depth, rows = tile_ref.shape[0], tile_ref.shape[1]
    right = lax.axis_index("gz") == 0
    even = lax.rem(lax.axis_index("gy"), 2) == 0
    turned_by = jnp.where(right, WIDE, 0)
    masks = [lane_mask(lambda lane: (((lane + turned_by) & 127) >> 2) == y) for y in range(rows)]
    for x in range(depth):
        parts = [jnp.zeros((16, 128), BF) for _ in range(4)]
        for y in range(rows):
            moved = pltpu.roll(tile_ref[x, y], 4 * y, 1) if y else tile_ref[x, y]
            parts[y % 4] = parts[y % 4] + moved * masks[y]
        total = (parts[0] + parts[1]) + (parts[2] + parts[3])
        z_ref[x] = pltpu.roll(total, turned_by, 1)
    first = jnp.where(even, rows - WIDE, 0)
    second = jnp.where(even, 0, rows - WIDE)
    for x in range(depth):
        a_ref[x * WIDE : (x + 1) * WIDE] = tile_ref[x, pl.ds(first, WIDE)]
        b_ref[x * WIDE : (x + 1) * WIDE] = tile_ref[x, pl.ds(second, WIDE)]


def weight_kernel(flip_x, w_ref, b_ref, t_ref):
    layers = w_ref.shape[0]
    zero = jnp.zeros((16, 16), BF)
    flipped = lax.axis_index("gx") == 1 if flip_x else None
    row = lax.broadcasted_iota(jnp.int32, (16, 16), 0)
    col = lax.broadcasted_iota(jnp.int32, (16, 16), 1)
    for layer in range(layers):
        for dz in range(3):
            for xo in range(2):
                for yo in range(2):
                    pieces = []
                    for xi in range(4):
                        for yi in range(4):
                            dx, dy = xi - xo, yi - yo
                            if 0 <= dx < 3 and 0 <= dy < 3:
                                at = jnp.where(flipped, 2 - dx, dx) if flip_x else dx
                                pieces.append(w_ref[layer, at, dy, dz])
                            else:
                                pieces.append(zero)
                    at_row = ((dz * 2 + xo) * 2 + yo) * 16
                    t_ref[layer, at_row : at_row + 16] = jnp.concatenate(pieces, 1)
        spread = jnp.broadcast_to(b_ref[layer : layer + 1, :].astype(F32), (16, 16))
        column = jnp.sum(jnp.where(row == col, spread, 0.0), axis=1, keepdims=True)
        t_ref[layer, 192:208] = jnp.broadcast_to(column, (16, 256)).astype(BF)


def layer_kernel(two_sided, counts, plan, n_raw, n_state, *refs):
    fills, steps, emits = plan
    raws, refs = refs[:n_raw], refs[n_raw:]
    halos, refs = refs[:n_raw], refs[n_raw:]
    mine_ref, other_ref = refs[:2]
    refs = refs[2 + n_state :]
    levels, strips, refs = refs[:4], refs[4:8], refs[8:]
    if emits:
        keep_ref, send_ref, t_ref, bias_ref, out_ref, sems = refs
    else:
        t_ref, bias_ref = refs
    depth, rows = raws[0].shape[0], raws[0].shape[1]
    ext_rows = rows + 2 * WIDE
    per = strips[0].shape[1] - 2
    segments = 128 // SEG
    blk = depth * WIDE + depth
    section = lax.axis_index("segment")
    gx, gy = lax.axis_index("gx"), lax.axis_index("gy")
    right = lax.axis_index("gz") == 0
    even = lax.rem(gy, 2) == 0
    top_ok = jnp.where(gy == 0, 0.0, 1.0).astype(F32)
    low_ok = jnp.where(gy == counts["gy"] - 1, 0.0, 1.0).astype(F32)
    prev_at = jnp.where(even, blk, 0)
    next_at = jnp.where(even, 0, blk)
    zero_tile = jnp.zeros((16, 128), BF)
    own_at = WIDE if two_sided else 0

    def flip(i):
        return i if two_sided else jnp.where(gx == 1, depth - 1 - i, i)

    if not n_state:
        for v, s in zip(levels, strips):
            for x in (0, 1):
                v[x] = jnp.zeros(v.shape[1:], BF)
                s[x] = jnp.zeros(s.shape[1:], BF)
        for x in range(2, levels[0].shape[0]):
            levels[0][x, 0] = zero_tile
            levels[0][x, ext_rows + 1] = zero_tile
            levels[2][x, 2] = zero_tile
            levels[2][x, ext_rows - 1] = zero_tile

    ahead = jnp.where(right, 3 * WIDE, 0)
    own_masks = [
        lane_mask(
            lambda lane: ((((lane + ahead) & 127) >> 4) == j) & (((lane + ahead) & 15) < 3 * WIDE)
        )
        for j in range(segments)
    ]
    halo_masks = [lane_mask(lambda lane: ((lane >> 4) == j) & ((lane & 15) < WIDE)) for j in range(segments)]
    own_turn = jnp.where(right, 3 * WIDE, WIDE)
    halo_turn = jnp.where(right, 3 * WIDE, 0)
    va, sa = levels[0], strips[0]

    for p, source, place in fills:
        i = flip(place)
        h = halos[source]
        q = p + 2
        va[q, 1 + WIDE : 1 + WIDE + rows] = raws[source][i]
        va[q, 1 : 1 + WIDE] = h[pl.ds(prev_at + i * WIDE, WIDE)]
        va[q, 1 + WIDE + rows : 1 + 2 * WIDE + rows] = h[pl.ds(next_at + i * WIDE, WIDE)]
        edge_prev = h[prev_at + depth * WIDE + i]
        edge_own = h[2 * blk + i]
        edge_next = h[next_at + depth * WIDE + i]
        for yo in range(per):
            own_sum, halo_sum = zero_tile, zero_tile
            for j in range(segments):
                r = per * j + yo
                if r >= ext_rows:
                    continue
                row = va[q, 1 + r]
                own_sum = own_sum + (pltpu.roll(row, SEG * j, 1) if j else row) * own_masks[j]
                if r < WIDE:
                    edge, lane = edge_prev, WIDE * (rows - WIDE + r)
                elif r < WIDE + rows:
                    edge, lane = edge_own, WIDE * (r - WIDE)
                else:
                    edge, lane = edge_next, WIDE * (r - WIDE - rows)
                by = (SEG * j - lane) % 128
                halo_sum = halo_sum + (pltpu.roll(edge, by, 1) if by else edge) * halo_masks[j]
            sa[q, 1 + yo] = pltpu.roll(own_sum, own_turn, 1) + pltpu.roll(halo_sum, halo_turn, 1)
        sa[q, 0] = pltpu.roll(sa[q, per], SEG, 1)
        sa[q, per + 1] = pltpu.roll(sa[q, 1], 128 - SEG, 1)

    for layer in range(2):
        t_ref[2 * section + layer] = mine_ref[layer]
        t_ref[2 * (1 - section) + layer] = other_ref[layer]
    for layer in range(4):
        one = t_ref[layer, 192:208, :128].astype(F32)
        for k in range(4):
            bias_ref[layer, 16 * k : 16 * (k + 1)] = one

    wide_lane = lax.broadcasted_iota(jnp.int32, (64, 128), 1)
    not_first = jnp.where(wide_lane == 0, 0.0, 1.0)
    not_last = jnp.where(wide_lane == 127, 0.0, 1.0)
    strip_lane = lax.broadcasted_iota(jnp.int32, (16, 128), 1) >> 4

    def strip_ok(yo):
        r = strip_lane * per + yo
        return jnp.where(r < WIDE, top_ok, jnp.where(r >= WIDE + rows, low_ok, 1.0))

    def group(layer, at):
        src, ssrc = levels[layer], strips[layer]
        last = layer == 3
        dst, sdst = (levels[0], strips[0]) if last else (levels[layer + 1], strips[layer + 1])
        r0, row_groups = ((0, ext_rows // 2), (2, ext_rows // 2 - 2), (2, ext_rows // 2 - 2), (WIDE, rows // 2))[layer]
        items = [(src, r0 + 2 * k, False) for k in range(row_groups)]
        items += [(ssrc, 2 * k, True) for k in range(per // 2)]
        half = len(items) // 2
        order = [[items[k], items[half + k]] for k in range(half)] + [[t] for t in items[2 * half :]]
        for pair in order:
            columns = [
                jnp.concatenate([ref[at + 1 + xi, r : r + 4].reshape(64, 128) for xi in range(4)], 0)
                for ref, r, _ in pair
            ]
            wide = jnp.concatenate(columns, 1) if len(columns) > 1 else columns[0]
            got = jnp.dot(t_ref[layer, :192], wide, preferred_element_type=F32)
            for k, (_, r, strip) in enumerate(pair):
                part = got[:, 128 * k : 128 * (k + 1)]
                a = part[64:128] + pltpu.roll(part[:64], 1, 1) * not_first
                a = a + pltpu.roll(part[128:], 127, 1) * not_last
                a = a + bias_ref[layer]
                a = jnp.maximum(a, 0.2 * a)
                for xo in range(2):
                    place = at + xo
                    if isinstance(place, int) and place < 0:
                        continue
                    for yo in range(2):
                        one = a[(2 * xo + yo) * 16 : (2 * xo + yo + 1) * 16]
                        if not last:
                            if strip:
                                one = one * strip_ok(r + yo)
                            elif r + yo < WIDE:
                                one = one * top_ok
                            elif r + yo >= WIDE + rows:
                                one = one * low_ok
                            if two_sided:
                                outside = ((place < WIDE) & (gx == 0)) | (
                                    (place >= WIDE + depth) & (gx == counts["gx"] - 1)
                                )
                                one = one * jnp.where(outside, 0.0, 1.0)
                        one = one.astype(BF)
                        if strip:
                            sdst[place + 2, r + yo + 1] = one
                            if r + yo == 0:
                                sdst[place + 2, per + 1] = pltpu.roll(one, 128 - SEG, 1)
                            if r + yo == per - 1:
                                sdst[place + 2, 0] = pltpu.roll(one, SEG, 1)
                        else:
                            dst[place + 2, r + yo + 1] = one

    def emit(part, places):
        turn = transposer()
        edge_turn = jnp.where(right, 0, 2 * WIDE)
        edge_ahead = jnp.where(right, WIDE, 0)
        edge_mask = lane_mask(lambda lane: ((lane + edge_ahead) & 127) < WIDE)
        inner_mask = lane_mask(lambda lane: ((lane + edge_ahead) & 127) >= WIDE)
        v, s = (levels[2], strips[2]) if part == 0 else (levels[0], strips[0])
        for i in places:
            p = own_at + i
            to = flip(i)
            starts = list(range(0, rows, 16))
            for k in range(0, len(starts), 2):
                some = starts[k : k + 2]
                blocks = []
                for y0 in some:
                    tiles = []
                    for y in range(y0, y0 + 16):
                        r = y + WIDE
                        j, yo = r // per, r % per
                        by = (128 - 3 * WIDE - SEG * j) % 128
                        edge = pltpu.roll(s[p + 2, yo + 1], by + edge_turn, 1)
                        tiles.append(v[p + 2, r + 1] * inner_mask + edge * edge_mask)
                    blocks.append(jnp.concatenate(tiles, 0))
                for y0, block in zip(some, swap_rows(turn, blocks)):
                    out_ref[part, :, to, y0 : y0 + 16] = block

    def copies(part):
        return (
            pltpu.make_async_copy(out_ref.at[part], keep_ref.at[section], sems.at[part]),
            pltpu.make_async_copy(out_ref.at[part], send_ref, sems.at[part]),
        )

    def move(part, finish):
        keep, send = copies(part)

        @pl.when(section == part)
        def _():
            (keep.wait if finish else keep.start)()

        @pl.when(section != part)
        def _():
            (send.wait if finish else send.start)()

    for step in steps:
        if step[0] == "emit":
            emit(step[1], range(depth))
            move(step[1], False)
        elif step[0] == "loop":
            _, layer, x0, n = step

            def body(g, carry):
                group(layer, x0 + 2 * g)
                return carry

            lax.fori_loop(0, n, body, 0)
        else:
            group(*step[1:])
    if emits:
        for part in range(2):
            move(part, True)


VMEM = pl.BlockSpec(memory_space=pltpu.VMEM)
ANY = pl.BlockSpec(memory_space=pl.ANY)


def shards(counts, features, weights, biases):
    gx, gy, gz = (counts[a] for a in ("gx", "gy", "gz"))
    two_sided = gx != 2
    section = lax.axis_index("segment")
    micro, chans, depth, rows, lanes = features.shape
    tiles = pl.pallas_call(
        tile_kernel,
        out_shape=jax.ShapeDtypeStruct((depth, rows, chans, lanes), BF),
        in_specs=[pl.BlockSpec(memory_space=pltpu.HBM)],
        out_specs=VMEM,
        scratch_shapes=[
            pltpu.VMEM((chans, depth, rows, lanes), BF),
            pltpu.SemaphoreType.DMA((depth,)),
        ],
        name="tiles",
        compiler_params=pltpu.CompilerParams(vmem_limit_bytes=4 << 20),
        cost_estimate=pl.CostEstimate(flops=4_000_000, bytes_accessed=1_000_000, transcendentals=0),
    )(features)

    def along_x(low, high):
        if not two_sided:
            return [lax.ppermute(low, "gx", swap_pairs(2))]
        up = [(i, i + 1) for i in range(gx - 1)]
        return [lax.ppermute(high, "gx", up), lax.ppermute(low, "gx", [(j, i) for i, j in up])]

    raws = along_x(tiles, tiles)
    edge_z, edge_a, edge_b = pl.pallas_call(
        pack_kernel,
        out_shape=(
            jax.ShapeDtypeStruct((depth, chans, lanes), BF),
            jax.ShapeDtypeStruct((depth * WIDE, chans, lanes), BF),
            jax.ShapeDtypeStruct((depth * WIDE, chans, lanes), BF),
        ),
        in_specs=[VMEM],
        out_specs=(VMEM,) * 3,
        name="pack",
        compiler_params=pltpu.CompilerParams(vmem_limit_bytes=4 << 20),
        cost_estimate=pl.CostEstimate(flops=4_000_000, bytes_accessed=1_000_000, transcendentals=0),
    )(tiles)
    from_z = lax.ppermute(edge_z, "gz", swap_pairs(gz))
    from_b = lax.ppermute(jnp.concatenate([edge_b, from_z]), "gy", shifted_pairs(gy))
    from_a = lax.ppermute(jnp.concatenate([edge_a, from_z]), "gy", swap_pairs(gy))
    halo = jnp.concatenate([from_a, from_b, from_z])
    halos = along_x(halo, halo)

    table = pl.pallas_call(
        functools.partial(weight_kernel, not two_sided),
        out_shape=jax.ShapeDtypeStruct((2, 208, 256), BF),
        in_specs=[VMEM] * 2,
        out_specs=VMEM,
        name="weights",
        compiler_params=pltpu.CompilerParams(vmem_limit_bytes=4 << 20),
        cost_estimate=pl.CostEstimate(flops=1_000_000, bytes_accessed=400_000, transcendentals=0),
    )(jnp.transpose(weights[0], (0, 3, 4, 5, 1, 2)), biases[0])
    other = lax.ppermute(table, "segment", swap_pairs(2))
    ext = depth + (2 * WIDE if two_sided else WIDE)
    ext_rows = rows + 2 * WIDE
    per = -(-ext_rows * SEG // 128)
    per += per % 2
    state = [jax.ShapeDtypeStruct((ext + 2, ext_rows + 2, chans, lanes), BF)] * 4
    state += [jax.ShapeDtypeStruct((ext + 2, per + 2, chans, lanes), BF)] * 4
    results = [
        jax.ShapeDtypeStruct((micro, chans, depth, rows, lanes), BF),
        jax.ShapeDtypeStruct((chans, depth, rows, lanes), BF),
    ]

    def stage(plan, blocks, edges, before):
        _, _, emits = plan
        n = len(blocks)
        return pl.pallas_call(
            functools.partial(layer_kernel, two_sided, counts, plan, n, len(before)),
            out_shape=state + (results if emits else []),
            in_specs=[VMEM] * (2 * n + 2 + len(before)),
            out_specs=[VMEM] * 8 + ([ANY, ANY] if emits else []),
            scratch_shapes=[pltpu.VMEM((4, 208, 256), BF), pltpu.VMEM((4, 64, 128), F32)]
            + ([pltpu.VMEM((2, chans, depth, rows, lanes), BF), pltpu.SemaphoreType.DMA((2,))] if emits else []),
            input_output_aliases={2 * n + 2 + k: k for k in range(len(before))},
            compiler_params=pltpu.CompilerParams(vmem_limit_bytes=24 << 20),
            cost_estimate=pl.CostEstimate(flops=2_000_000_000, bytes_accessed=4_000_000, transcendentals=0),
        )(*blocks, *edges, table, other, *before)

    def chain(k):
        return [("one", layer, 2 * k - 1 - layer) for layer in range(4) if 2 * k - layer >= 0]

    if two_sided:
        fills = [(p, 1, depth - WIDE + p) for p in range(WIDE)]
        fills += [(WIDE + p, 0, p) for p in range(depth)]
        fills += [(WIDE + depth + p, 2, p) for p in range(WIDE)]
        steps = []
        for layer in range(4):
            steps.append(("loop", layer, layer + 1, (ext - 2 * layer - 2) // 2))
            if layer % 2:
                steps.append(("emit", layer // 2))
        *_, keep, send = stage((fills, steps, True), [tiles, *raws], [halo, *halos], [])
    else:
        near = [(p, 0, p) for p in range(depth)]
        early = stage((near, chain(0) + chain(1), False), [tiles], [halo], [])
        far = [(depth + p, 0, p) for p in range(WIDE)]
        steps = chain(2) + [("emit", 0)] + chain(3) + [("emit", 1)]
        *_, keep, send = stage((far, steps, True), raws, halos, early)
    got = lax.ppermute(send, "segment", swap_pairs(2))
    return lax.dynamic_update_index_in_dim(keep, got, 1 - section, 0)[None]


def solution(mesh):
    placed = (
        P(None, None, "gx", "gy", "gz"),
        P("segment", None, None, None, None, None, None),
        P("segment", None, None),
    )

    def step(*args):
        return shards(dict(mesh.shape), *args)

    return jax.shard_map(
        step,
        mesh=mesh,
        in_specs=placed,
        out_specs=P("segment", None, None, "gx", "gy", "gz"),
        check_vma=False,
    )
```

```python
import functools

import jax
import jax.numpy as jnp
from jax import lax
from jax.experimental import pallas as pl
from jax.experimental.pallas import tpu as pltpu
from jax.sharding import PartitionSpec as P


WIDE = 4
SEG = 16
BF = jnp.bfloat16
F32 = jnp.float32


def swap_pairs(size):
    return [(i, i ^ 1) for i in range(size) if i ^ 1 < size]


def shifted_pairs(size):
    up = [(i, i + 1) for i in range(1, size - 1, 2)]
    return up + [(j, i) for i, j in up]


def transposer():
    row = lax.broadcasted_iota(jnp.int32, (256, 256), 0)
    col = lax.broadcasted_iota(jnp.int32, (256, 256), 1)
    hit = ((row >> 4) == (col & 15)) & ((row & 15) == (col >> 4))
    return jnp.where(hit, 1.0, 0.0).astype(BF)


def lane_mask(test):
    lane = lax.broadcasted_iota(jnp.int32, (16, 128), 1)
    return jnp.where(test(lane), 1.0, 0.0).astype(BF)


def swap_rows(turn, blocks):
    wide = jnp.concatenate(blocks, 1) if len(blocks) > 1 else blocks[0]
    turned = jnp.dot(turn, wide, preferred_element_type=F32).astype(BF)
    return [turned[:, k * 128 : (k + 1) * 128].reshape(16, 16, 128) for k in range(len(blocks))]


def fill_table(flip_x, w_ref, b_ref, t_ref):
    zero = jnp.zeros((16, 16), BF)
    flipped = lax.axis_index("gx") == 1 if flip_x else None
    row = lax.broadcasted_iota(jnp.int32, (16, 16), 0)
    col = lax.broadcasted_iota(jnp.int32, (16, 16), 1)
    for layer in range(w_ref.shape[0]):
        for dz in range(3):
            for xo in range(2):
                for yo in range(2):
                    pieces = []
                    for xi in range(4):
                        for yi in range(4):
                            dx, dy = xi - xo, yi - yo
                            if 0 <= dx < 3 and 0 <= dy < 3:
                                at = jnp.where(flipped, 2 - dx, dx) if flip_x else dx
                                pieces.append(w_ref[layer, at, dy, dz])
                            else:
                                pieces.append(zero)
                    at_row = ((dz * 2 + xo) * 2 + yo) * 16
                    t_ref[layer, at_row : at_row + 16] = jnp.concatenate(pieces, 1)
        spread = jnp.broadcast_to(b_ref[layer : layer + 1, :].astype(F32), (16, 16))
        column = jnp.sum(jnp.where(row == col, spread, 0.0), axis=1, keepdims=True)
        t_ref[layer, 192:208] = jnp.broadcast_to(column, (16, 256)).astype(BF)


def pack_kernel(flip_x, x_hbm, w_hbm, b_hbm, tile_ref, z_ref, a_ref, b_ref, t_ref, x_ref, w_ref, bias_ref, sems):
    depth, rows = tile_ref.shape[0], tile_ref.shape[1]
    section = lax.axis_index("segment")
    chans = x_ref.shape[0]
    small = [
        pltpu.make_async_copy(w_hbm, w_ref, sems.at[chans]),
        pltpu.make_async_copy(b_hbm, bias_ref, sems.at[chans + 1]),
    ]
    copies = [pltpu.make_async_copy(x_hbm.at[section, c], x_ref.at[c], sems.at[c]) for c in range(chans)]
    for copy in small + copies:
        copy.start()
    right = lax.axis_index("gz") == 0
    even = lax.rem(lax.axis_index("gy"), 2) == 0
    turned_by = jnp.where(right, WIDE, 0)
    turn = transposer()
    masks = [lane_mask(lambda lane: (((lane + turned_by) & 127) >> 2) == y) for y in range(rows)]
    first = jnp.where(even, rows - WIDE, 0)
    second = jnp.where(even, 0, rows - WIDE)
    for copy in small:
        copy.wait()
    fill_table(flip_x, w_ref, bias_ref, t_ref)
    for copy in copies:
        copy.wait()
    for x in range(depth):
        tiles = []
        for y0 in range(0, rows, 32):
            starts = range(y0, min(y0 + 32, rows), 16)
            for at, block in zip(starts, swap_rows(turn, [x_ref[:, x, k : k + 16, :].reshape(256, 128) for k in starts])):
                tile_ref[x, at : at + 16] = block
                tiles += [block[k] for k in range(16)]
        parts = [jnp.zeros((16, 128), BF) for _ in range(4)]
        for y, tile in enumerate(tiles):
            moved = pltpu.roll(tile, 4 * y, 1) if y else tile
            parts[y % 4] = parts[y % 4] + moved * masks[y]
        total = (parts[0] + parts[1]) + (parts[2] + parts[3])
        z_ref[x] = pltpu.roll(total, turned_by, 1)
        a_ref[x] = tile_ref[x, pl.ds(first, WIDE)]
        b_ref[x] = tile_ref[x, pl.ds(second, WIDE)]


def layer_kernel(two_sided, counts, plan, n_raw, n_edge, n_held, half_ids, *refs):
    fills, steps, _ = plan
    raws, refs = refs[:n_raw], refs[n_raw:]
    halos, refs = refs[:n_edge], refs[n_edge:]
    begins = n_held == 0
    (one_ref, two_ref), refs = refs[:2], refs[2:]
    held, refs = refs[:n_held], refs[n_held:]
    levels, strips, refs = refs[:4], refs[4:8], refs[8:]
    if begins:
        mine_ref, other_ref = one_ref, two_ref
        (t_ref, bias_ref), refs = refs[:2], refs[2:]
    else:
        t_ref, bias_ref = one_ref, two_ref
    halves, refs = refs[: len(half_ids)], refs[len(half_ids) :]
    sem = refs[-1]
    rows = levels[0].shape[1] - 2 - 2 * WIDE
    depth = plan[2]
    ext_rows = rows + 2 * WIDE
    per = strips[0].shape[1] - 2
    segments = 128 // SEG
    section = lax.axis_index("segment")
    gx, gy = lax.axis_index("gx"), lax.axis_index("gy")
    right = lax.axis_index("gz") == 0
    even = lax.rem(gy, 2) == 0
    top_ok = jnp.where(gy == 0, 0.0, 1.0).astype(F32)
    low_ok = jnp.where(gy == counts["gy"] - 1, 0.0, 1.0).astype(F32)
    prev_at = jnp.where(even, WIDE + 1, 0)
    next_at = jnp.where(even, 0, WIDE + 1)
    zero_tile = jnp.zeros((16, 128), BF)
    own_at = WIDE if two_sided else 0

    def flip(i, size):
        return i if two_sided else jnp.where(gx == 1, size - 1 - i, i)

    if begins:
        for v, s in zip(levels, strips):
            for x in (0, 1):
                v[x] = jnp.zeros(v.shape[1:], BF)
                s[x] = jnp.zeros(s.shape[1:], BF)
        for x in range(2, levels[0].shape[0]):
            levels[0][x, 0] = zero_tile
            levels[0][x, ext_rows + 1] = zero_tile
            levels[2][x, 2] = zero_tile
            levels[2][x, ext_rows - 1] = zero_tile

    ahead = jnp.where(right, 3 * WIDE, 0)
    own_masks = [
        lane_mask(
            lambda lane: ((((lane + ahead) & 127) >> 4) == j) & (((lane + ahead) & 15) < 3 * WIDE)
        )
        for j in range(segments)
    ]
    halo_masks = [lane_mask(lambda lane: ((lane >> 4) == j) & ((lane & 15) < WIDE)) for j in range(segments)]
    own_turn = jnp.where(right, 3 * WIDE, WIDE)
    halo_turn = jnp.where(right, 3 * WIDE, 0)
    va, sa = levels[0], strips[0]

    for p, source, place, edge_place in fills:
        q = p + 2
        if place is not None:
            va[q, 1 + WIDE : 1 + WIDE + rows] = raws[source][flip(place, depth)]
        if edge_place is None:
            continue
        h = halos[source]
        i = flip(edge_place, h.shape[0])
        va[q, 1 : 1 + WIDE] = h[i, pl.ds(prev_at, WIDE)]
        va[q, 1 + WIDE + rows : 1 + 2 * WIDE + rows] = h[i, pl.ds(next_at, WIDE)]
        edge_prev = h[i, prev_at + WIDE]
        edge_own = h[i, 2 * WIDE + 2]
        edge_next = h[i, next_at + WIDE]
        for yo in range(per):
            own_sum, halo_sum = zero_tile, zero_tile
            for j in range(segments):
                r = per * j + yo
                if r >= ext_rows:
                    continue
                row = va[q, 1 + r]
                own_sum = own_sum + (pltpu.roll(row, SEG * j, 1) if j else row) * own_masks[j]
                if r < WIDE:
                    edge, lane = edge_prev, WIDE * (rows - WIDE + r)
                elif r < WIDE + rows:
                    edge, lane = edge_own, WIDE * (r - WIDE)
                else:
                    edge, lane = edge_next, WIDE * (r - WIDE - rows)
                by = (SEG * j - lane) % 128
                halo_sum = halo_sum + (pltpu.roll(edge, by, 1) if by else edge) * halo_masks[j]
            sa[q, 1 + yo] = pltpu.roll(own_sum, own_turn, 1) + pltpu.roll(halo_sum, halo_turn, 1)
        sa[q, 0] = pltpu.roll(sa[q, per], SEG, 1)
        sa[q, per + 1] = pltpu.roll(sa[q, 1], 128 - SEG, 1)

    if begins:
        for layer in range(2):
            t_ref[2 * section + layer] = mine_ref[layer]
            t_ref[2 * (1 - section) + layer] = other_ref[layer]
        for layer in range(4):
            one = t_ref[layer, 192:208, :128].astype(F32)
            for k in range(4):
                bias_ref[layer, 16 * k : 16 * (k + 1)] = one

    wide_lane = lax.broadcasted_iota(jnp.int32, (64, 128), 1)
    not_first = jnp.where(wide_lane == 0, 0.0, 1.0)
    not_last = jnp.where(wide_lane == 127, 0.0, 1.0)
    strip_lane = lax.broadcasted_iota(jnp.int32, (16, 128), 1) >> 4

    def strip_ok(yo):
        r = strip_lane * per + yo
        return jnp.where(r < WIDE, top_ok, jnp.where(r >= WIDE + rows, low_ok, 1.0))

    def group(layer, at, part=None):
        src, ssrc = levels[layer], strips[layer]
        last = layer == 3
        dst, sdst = (levels[0], strips[0]) if last else (levels[layer + 1], strips[layer + 1])
        r0, row_groups = ((0, ext_rows // 2), (2, ext_rows // 2 - 2), (2, ext_rows // 2 - 2), (WIDE, rows // 2))[layer]
        margin = WIDE + 2 * (layer + 1)
        inner = [margin <= r0 + 2 * k < ext_rows - margin for k in range(row_groups)]
        items = [(src, r0 + 2 * k, False) for k in range(row_groups) if part is None or inner[k] == (part == 0)]
        if part != 0:
            items += [(ssrc, 2 * k, True) for k in range(per // 2)]
        half = len(items) // 2
        order = [[items[k], items[half + k]] for k in range(half)] + [[t] for t in items[2 * half :]]
        for pair in order:
            columns = [
                jnp.concatenate([ref[at + 1 + xi, r : r + 4].reshape(64, 128) for xi in range(4)], 0)
                for ref, r, _ in pair
            ]
            wide = jnp.concatenate(columns, 1) if len(columns) > 1 else columns[0]
            got = jnp.dot(t_ref[layer, :192], wide, preferred_element_type=F32)
            for k, (_, r, strip) in enumerate(pair):
                part = got[:, 128 * k : 128 * (k + 1)]
                a = part[64:128] + pltpu.roll(part[:64], 1, 1) * not_first
                a = a + pltpu.roll(part[128:], 127, 1) * not_last
                a = a + bias_ref[layer]
                a = jnp.maximum(a, 0.2 * a)
                for xo in range(2):
                    place = at + xo
                    if isinstance(place, int) and place < 0:
                        continue
                    for yo in range(2):
                        one = a[(2 * xo + yo) * 16 : (2 * xo + yo + 1) * 16]
                        if not last:
                            if strip:
                                one = one * strip_ok(r + yo)
                            elif r + yo < WIDE:
                                one = one * top_ok
                            elif r + yo >= WIDE + rows:
                                one = one * low_ok
                            if two_sided:
                                outside = ((place < WIDE) & (gx == 0)) | (
                                    (place >= WIDE + depth) & (gx == counts["gx"] - 1)
                                )
                                one = one * jnp.where(outside, 0.0, 1.0)
                        one = one.astype(BF)
                        if strip:
                            sdst[place + 2, r + yo + 1] = one
                            if r + yo == 0:
                                sdst[place + 2, per + 1] = pltpu.roll(one, 128 - SEG, 1)
                            if r + yo == per - 1:
                                sdst[place + 2, 0] = pltpu.roll(one, SEG, 1)
                        else:
                            dst[place + 2, r + yo + 1] = one

    def emit(part, half):
        turn = transposer()
        edge_turn = jnp.where(right, 0, 2 * WIDE)
        edge_ahead = jnp.where(right, WIDE, 0)
        edge_mask = lane_mask(lambda lane: ((lane + edge_ahead) & 127) < WIDE)
        inner_mask = lane_mask(lambda lane: ((lane + edge_ahead) & 127) >= WIDE)
        v, s = (levels[2], strips[2]) if part == 0 else (levels[0], strips[0])
        out_ref = halves[half_ids.index(half)]
        role = jnp.where(section == part, 0, 1)
        size = out_ref.shape[2]
        for i in range(size):
            p = own_at + half * size + i
            to = flip(i, size)
            starts = list(range(0, rows, 16))
            for k in range(0, len(starts), 2):
                some = starts[k : k + 2]
                blocks = []
                for y0 in some:
                    tiles = []
                    for y in range(y0, y0 + 16):
                        r = y + WIDE
                        j, yo = r // per, r % per
                        by = (128 - 3 * WIDE - SEG * j) % 128
                        edge = pltpu.roll(s[p + 2, yo + 1], by + edge_turn, 1)
                        tiles.append(v[p + 2, r + 1] * inner_mask + edge * edge_mask)
                    blocks.append(jnp.concatenate(tiles, 0))
                for y0, block in zip(some, swap_rows(turn, blocks)):
                    out_ref[role, :, to, y0 : y0 + 16] = block

    def keep(finish):
        source = halves[0] if begins else held[8]
        size = source.shape[2]
        start = flip(0, 2) * size
        copy = pltpu.make_async_copy(source.at[0], refs[0].at[section, :, pl.ds(start, size)], sem)
        (copy.wait if finish else copy.start)()

    for step in steps:
        if step[0] == "emit":
            emit(*step[1:])
        elif step[0] == "keep":
            keep(step[1])
        elif step[0] == "loop":
            _, layer, x0, n = step

            def body(g, carry):
                group(layer, x0 + 2 * g)
                return carry

            lax.fori_loop(0, n, body, 0)
        else:
            group(*step[1:])


def place_kernel(two_sided, moves, *refs):
    sources, out_ref, sems = refs[1:-2], refs[-2], refs[-1]
    section = lax.axis_index("segment")
    flipped = False if two_sided else lax.axis_index("gx") == 1
    copies = []
    for k, (own, half) in enumerate(moves):
        source = sources[k].at[0] if own else sources[k]
        size = source.shape[1]
        start = half * size if two_sided else jnp.where(flipped, 1 - half, half) * size
        place = out_ref.at[section if own else 1 - section, :, pl.ds(start, size)]
        copies.append(pltpu.make_async_copy(source, place, sems.at[k]))
    for copy in copies:
        copy.start()
    for copy in copies:
        copy.wait()


VMEM = pl.BlockSpec(memory_space=pltpu.VMEM)
ANY = pl.BlockSpec(memory_space=pl.ANY)


def shards(counts, features, weights, biases):
    gx, gy, gz = (counts[a] for a in ("gx", "gy", "gz"))
    two_sided = gx != 2
    micro, chans, depth, rows, lanes = features.shape
    edge = jax.ShapeDtypeStruct((depth, WIDE, chans, lanes), BF)
    hbm = pl.BlockSpec(memory_space=pltpu.HBM)
    in_hbm = lambda v: pltpu.with_memory_space_constraint(v, pltpu.HBM)
    tiles, edge_z, edge_a, edge_b, table = pl.pallas_call(
        functools.partial(pack_kernel, not two_sided),
        out_shape=(
            jax.ShapeDtypeStruct((depth, rows, chans, lanes), BF),
            jax.ShapeDtypeStruct((depth, chans, lanes), BF),
            edge,
            edge,
            jax.ShapeDtypeStruct((2, 208, 256), BF),
        ),
        in_specs=[hbm] * 3,
        out_specs=(VMEM,) * 5,
        scratch_shapes=[
            pltpu.VMEM((chans, depth, rows, lanes), BF),
            pltpu.VMEM((2, 3, 3, 3, chans, chans), BF),
            pltpu.VMEM((2, chans), BF),
            pltpu.SemaphoreType.DMA((chans + 2,)),
        ],
        name="pack",
        compiler_params=pltpu.CompilerParams(vmem_limit_bytes=4 << 20),
        cost_estimate=pl.CostEstimate(flops=4_000_000, bytes_accessed=1_000_000, transcendentals=0),
    )(in_hbm(features), in_hbm(jnp.transpose(weights[0], (0, 3, 4, 5, 1, 2))), in_hbm(biases[0]))

    def along_x(low, high):
        if not two_sided:
            return [lax.ppermute(low, "gx", swap_pairs(2))]
        up = [(i, i + 1) for i in range(gx - 1)]
        return [lax.ppermute(high, "gx", up), lax.ppermute(low, "gx", [(j, i) for i, j in up])]

    raws = along_x(tiles, tiles)
    from_z = lax.ppermute(edge_z, "gz", swap_pairs(gz))
    at_z = from_z[:, None]
    from_b = lax.ppermute(
        jnp.concatenate([edge_b, at_z], 1), "gy", shifted_pairs(gy)
    )
    from_a = lax.ppermute(jnp.concatenate([edge_a, at_z], 1), "gy", swap_pairs(gy))
    halo = jnp.concatenate([from_a, from_b, at_z], 1)
    half = depth // 2
    if two_sided:
        halos = along_x(halo, halo)
    else:
        start = jnp.where(lax.axis_index("gx") == 0, half, 0)
        near_halo = along_x(lax.dynamic_slice_in_dim(halo, start, half, 0), None)
        far_halo = along_x(lax.dynamic_slice_in_dim(halo, half - start, half, 0), None)

    other = lax.ppermute(table, "segment", swap_pairs(2))
    ext = depth + (2 * WIDE if two_sided else WIDE)
    ext_rows = rows + 2 * WIDE
    per = -(-ext_rows * SEG // 128)
    per += per % 2
    state = [jax.ShapeDtypeStruct((ext + 2, ext_rows + 2, chans, lanes), BF)] * 4
    state += [jax.ShapeDtypeStruct((ext + 2, per + 2, chans, lanes), BF)] * 4
    half_shape = jax.ShapeDtypeStruct((2, chans, half, rows, lanes), BF)
    keep_shape = jax.ShapeDtypeStruct((micro, chans, depth, rows, lanes), BF)

    def stage(plan, blocks, edges, pair, before=(), aliases=(), half_ids=(), keeps=False):
        n = len(blocks)
        start = n + len(edges) + 2
        shapes = list(state)
        if not before:
            shapes += [jax.ShapeDtypeStruct((4, 208, 256), BF), jax.ShapeDtypeStruct((4, 64, 128), F32)]
        shapes += [half_shape] * len(half_ids)
        return pl.pallas_call(
            functools.partial(layer_kernel, two_sided, counts, (*plan, depth), n, len(edges), len(before), half_ids),
            out_shape=shapes + ([keep_shape] if keeps else []),
            in_specs=[VMEM] * (start + len(before)),
            out_specs=[VMEM] * len(shapes) + ([ANY] if keeps else []),
            scratch_shapes=[pltpu.SemaphoreType.DMA],
            input_output_aliases={start + i: o for i, o in aliases},
            compiler_params=pltpu.CompilerParams(vmem_limit_bytes=24 << 20),
            cost_estimate=pl.CostEstimate(flops=2_000_000_000, bytes_accessed=4_000_000, transcendentals=0),
        )(*blocks, *edges, *pair, *before)

    def place(whole, sources, moves):
        return pl.pallas_call(
            functools.partial(place_kernel, two_sided, moves),
            out_shape=keep_shape,
            in_specs=[ANY] + [VMEM] * len(sources),
            out_specs=ANY,
            scratch_shapes=[pltpu.SemaphoreType.DMA((len(sources),))],
            input_output_aliases={0: 0},
            name="place",
            compiler_params=pltpu.CompilerParams(vmem_limit_bytes=2 << 20),
            cost_estimate=pl.CostEstimate(flops=0, bytes_accessed=500_000, transcendentals=0),
        )(whole, *sources)

    def chain(k, part=None):
        return [("one", layer, 2 * k - 1 - layer, part) for layer in range(4) if 2 * k - layer >= 0]

    if two_sided:
        fills = [(p, 1, depth - WIDE + p, depth - WIDE + p) for p in range(WIDE)]
        fills += [(WIDE + p, 0, p, p) for p in range(depth)]
        fills += [(WIDE + depth + p, 2, p, p) for p in range(WIDE)]
        steps = []
        for layer in range(4):
            steps.append(("loop", layer, layer + 1, (ext - 2 * layer - 2) // 2))
            if layer % 2:
                steps += [("emit", layer // 2, 0), ("emit", layer // 2, 1)]
        steps += [("keep", False), ("keep", True)]
        *_, first, second, whole = stage(
            (fills, steps), [tiles, *raws], [halo, *halos], (table, other), half_ids=(0, 1), keeps=True
        )
    else:
        same = [(k, k) for k in range(8)]
        fills = [(p, 0, p, None) for p in range(depth)]
        steps = chain(0, 0) + chain(1, 0)
        *state_now, t, bias = stage((fills, steps), [tiles], [], (table, other))
        fills = [(p, 0, None, p) for p in range(depth)]
        steps = chain(0, 1) + chain(1, 1) + [("emit", 0, 0)]
        *state_now, first = stage((fills, steps), [], [halo], (t, bias), state_now, same, (0,))
        fills = [(depth + p, 0, p, p) for p in range(half)]
        steps = chain(2)[:2] + [("emit", 0, 1)] + chain(2)[2:] + [("emit", 1, 0)]
        *state_now, first, second = stage(
            (fills, steps), raws, near_halo, (t, bias), [*state_now, first], same + [(8, 8)], (0, 1)
        )
        fills = [(depth + p, 0, p, p - half) for p in range(half, WIDE)]
        steps = [("keep", False)] + chain(3) + [("emit", 1, 1), ("keep", True)]
        *_, second, whole = stage(
            (fills, steps), raws, far_halo, (t, bias), [*state_now, first, second], same + [(9, 8)], (1,), True
        )

    got_first = lax.ppermute(first[1], "segment", swap_pairs(2))
    got_second = lax.ppermute(second[1], "segment", swap_pairs(2))
    whole = place(whole, [second, got_first], ((True, 1), (False, 0)))
    return place(whole, [got_second], ((False, 1),))[None]


def solution(mesh):
    placed = (
        P(None, None, "gx", "gy", "gz"),
        P("segment", None, None, None, None, None, None),
        P("segment", None, None),
    )

    def step(*args):
        return shards(dict(mesh.shape), *args)

    return jax.shard_map(
        step,
        mesh=mesh,
        in_specs=placed,
        out_specs=P("segment", None, None, "gx", "gy", "gz"),
        check_vma=False,
    )
```

```python
import functools
import itertools

import jax
import jax.numpy as jnp
from jax import lax
from jax.experimental import pallas as pl
from jax.experimental.pallas import tpu as pltpu
from jax.sharding import PartitionSpec as P


WIDE = 4
LAG = 4
SEG = 16
BF = jnp.bfloat16
F32 = jnp.float32


def swap_pairs(size):
    return [(i, i ^ 1) for i in range(size) if i ^ 1 < size]


def shifted_pairs(size):
    up = [(i, i + 1) for i in range(1, size - 1, 2)]
    return up + [(j, i) for i, j in up]


def transposer():
    row = lax.broadcasted_iota(jnp.int32, (256, 256), 0)
    col = lax.broadcasted_iota(jnp.int32, (256, 256), 1)
    hit = ((row >> 4) == (col & 15)) & ((row & 15) == (col >> 4))
    return jnp.where(hit, 1.0, 0.0).astype(BF)


def lane_mask(test):
    lane = lax.broadcasted_iota(jnp.int32, (16, 128), 1)
    return jnp.where(test(lane), 1.0, 0.0).astype(BF)


def swap_rows(turn, blocks):
    wide = jnp.concatenate(blocks, 1) if len(blocks) > 1 else blocks[0]
    turned = jnp.dot(turn, wide, preferred_element_type=F32).astype(BF)
    return [turned[:, k * 128 : (k + 1) * 128].reshape(16, 16, 128) for k in range(len(blocks))]


def fill_table(flip_x, w_ref, b_ref, t_ref):
    zero = jnp.zeros((16, 16), BF)
    flipped = lax.axis_index("gx") == 1 if flip_x else None
    row = lax.broadcasted_iota(jnp.int32, (16, 16), 0)
    col = lax.broadcasted_iota(jnp.int32, (16, 16), 1)
    for layer in range(w_ref.shape[0]):
        for dz in range(3):
            for xo in range(2):
                for yo in range(2):
                    pieces = []
                    for xi in range(4):
                        for yi in range(4):
                            dx, dy = xi - xo, yi - yo
                            if 0 <= dx < 3 and 0 <= dy < 3:
                                at = jnp.where(flipped, 2 - dx, dx) if flip_x else dx
                                pieces.append(w_ref[layer, at, dy, dz])
                            else:
                                pieces.append(zero)
                    at_row = ((dz * 2 + xo) * 2 + yo) * 16
                    t_ref[layer, at_row : at_row + 16] = jnp.concatenate(pieces, 1)
        spread = jnp.broadcast_to(b_ref[layer : layer + 1, :].astype(F32), (16, 16))
        column = jnp.sum(jnp.where(row == col, spread, 0.0), axis=1, keepdims=True)
        t_ref[layer, 192:208] = jnp.broadcast_to(column, (16, 256)).astype(BF)


def pack_kernel(flip_x, x_hbm, w_hbm, b_hbm, tile_ref, z_ref, a_ref, b_ref, t_ref, x_ref, w_ref, bias_ref, sems):
    depth, rows = tile_ref.shape[0], tile_ref.shape[1]
    section = lax.axis_index("segment")
    chans = x_ref.shape[0]
    small = [
        pltpu.make_async_copy(w_hbm, w_ref, sems.at[chans]),
        pltpu.make_async_copy(b_hbm, bias_ref, sems.at[chans + 1]),
    ]
    copies = [pltpu.make_async_copy(x_hbm.at[section, c], x_ref.at[c], sems.at[c]) for c in range(chans)]
    for copy in small + copies:
        copy.start()
    right = lax.axis_index("gz") == 0
    even = lax.rem(lax.axis_index("gy"), 2) == 0
    turned_by = jnp.where(right, WIDE, 0)
    turn = transposer()
    masks = [lane_mask(lambda lane: (((lane + turned_by) & 127) >> 2) == y) for y in range(rows)]
    first = jnp.where(even, rows - WIDE, 0)
    second = jnp.where(even, 0, rows - WIDE)
    for copy in small:
        copy.wait()
    fill_table(flip_x, w_ref, bias_ref, t_ref)
    for copy in copies:
        copy.wait()
    for x in range(depth):
        tiles = []
        for y0 in range(0, rows, 32):
            starts = range(y0, min(y0 + 32, rows), 16)
            for at, block in zip(starts, swap_rows(turn, [x_ref[:, x, k : k + 16, :].reshape(256, 128) for k in starts])):
                tile_ref[x, at : at + 16] = block
                tiles += [block[k] for k in range(16)]
        parts = [jnp.zeros((16, 128), BF) for _ in range(4)]
        for y, tile in enumerate(tiles):
            moved = pltpu.roll(tile, 4 * y, 1) if y else tile
            parts[y % 4] = parts[y % 4] + moved * masks[y]
        total = (parts[0] + parts[1]) + (parts[2] + parts[3])
        z_ref[x] = pltpu.roll(total, turned_by, 1)
        a_ref[x] = tile_ref[x, pl.ds(first, WIDE)]
        b_ref[x] = tile_ref[x, pl.ds(second, WIDE)]


def layer_kernel(two_sided, counts, plan, n_raw, n_edge, n_held, half_ids, *refs):
    fills, steps, _ = plan
    raws, refs = refs[:n_raw], refs[n_raw:]
    halos, refs = refs[:n_edge], refs[n_edge:]
    begins = n_held == 0
    (one_ref, two_ref), refs = refs[:2], refs[2:]
    refs = refs[n_held:]
    levels, strips, refs = refs[:4], refs[4:8], refs[8:]
    if begins:
        mine_ref, other_ref = one_ref, two_ref
        (t_ref, bias_ref), refs = refs[:2], refs[2:]
    else:
        t_ref, bias_ref = one_ref, two_ref
    halves = refs
    rows = levels[0].shape[1] - 2 - 2 * WIDE
    depth = plan[2]
    ext_rows = rows + 2 * WIDE
    per = strips[0].shape[1] - 2
    segments = 128 // SEG
    section = lax.axis_index("segment")
    gx, gy = lax.axis_index("gx"), lax.axis_index("gy")
    right = lax.axis_index("gz") == 0
    even = lax.rem(gy, 2) == 0
    top_ok = jnp.where(gy == 0, 0.0, 1.0).astype(F32)
    low_ok = jnp.where(gy == counts["gy"] - 1, 0.0, 1.0).astype(F32)
    prev_at = jnp.where(even, WIDE + 1, 0)
    next_at = jnp.where(even, 0, WIDE + 1)
    zero_tile = jnp.zeros((16, 128), BF)
    own_at = WIDE if two_sided else 0

    def flip(i, size):
        return i if two_sided else jnp.where(gx == 1, size - 1 - i, i)

    if begins:
        for v, s in zip(levels, strips):
            for x in (0, 1):
                v[x] = jnp.zeros(v.shape[1:], BF)
                s[x] = jnp.zeros(s.shape[1:], BF)
        for x in range(2, levels[0].shape[0]):
            levels[0][x, 0] = zero_tile
            levels[0][x, ext_rows + 1] = zero_tile
            levels[2][x, 2] = zero_tile
            levels[2][x, ext_rows - 1] = zero_tile

    ahead = jnp.where(right, 3 * WIDE, 0)
    own_masks = [
        lane_mask(
            lambda lane: ((((lane + ahead) & 127) >> 4) == j) & (((lane + ahead) & 15) < 3 * WIDE)
        )
        for j in range(segments)
    ]
    halo_masks = [lane_mask(lambda lane: ((lane >> 4) == j) & ((lane & 15) < WIDE)) for j in range(segments)]
    own_turn = jnp.where(right, 3 * WIDE, WIDE)
    halo_turn = jnp.where(right, 3 * WIDE, 0)
    va, sa = levels[0], strips[0]

    def fill(p, source, place, edge_place):
        q = p + 2
        if place is not None:
            va[q, 1 + WIDE : 1 + WIDE + rows] = raws[source][flip(place, depth)]
        if edge_place is None:
            return
        h = halos[source]
        i = flip(edge_place, h.shape[0])
        va[q, 1 : 1 + WIDE] = h[i, pl.ds(prev_at, WIDE)]
        va[q, 1 + WIDE + rows : 1 + 2 * WIDE + rows] = h[i, pl.ds(next_at, WIDE)]
        yield
        edge_prev = h[i, prev_at + WIDE]
        edge_own = h[i, 2 * WIDE + 2]
        edge_next = h[i, next_at + WIDE]
        for yo in range(per):
            own_sum, halo_sum = zero_tile, zero_tile
            for j in range(segments):
                r = per * j + yo
                if r >= ext_rows:
                    continue
                row = va[q, 1 + r]
                own_sum = own_sum + (pltpu.roll(row, SEG * j, 1) if j else row) * own_masks[j]
                if r < WIDE:
                    edge, lane = edge_prev, WIDE * (rows - WIDE + r)
                elif r < WIDE + rows:
                    edge, lane = edge_own, WIDE * (r - WIDE)
                else:
                    edge, lane = edge_next, WIDE * (r - WIDE - rows)
                by = (SEG * j - lane) % 128
                halo_sum = halo_sum + (pltpu.roll(edge, by, 1) if by else edge) * halo_masks[j]
            sa[q, 1 + yo] = pltpu.roll(own_sum, own_turn, 1) + pltpu.roll(halo_sum, halo_turn, 1)
            yield
        sa[q, 0] = pltpu.roll(sa[q, per], SEG, 1)
        sa[q, per + 1] = pltpu.roll(sa[q, 1], 128 - SEG, 1)

    if begins:
        for layer in range(2):
            t_ref[2 * section + layer] = mine_ref[layer]
            t_ref[2 * (1 - section) + layer] = other_ref[layer]
        for layer in range(4):
            one = t_ref[layer, 192:208, :128].astype(F32)
            for k in range(4):
                bias_ref[layer, 16 * k : 16 * (k + 1)] = one

    wide_lane = lax.broadcasted_iota(jnp.int32, (64, 128), 1)
    not_first = jnp.where(wide_lane == 0, 0.0, 1.0)
    not_last = jnp.where(wide_lane == 127, 0.0, 1.0)
    strip_lane = lax.broadcasted_iota(jnp.int32, (16, 128), 1) >> 4

    def strip_ok(yo):
        r = strip_lane * per + yo
        return jnp.where(r < WIDE, top_ok, jnp.where(r >= WIDE + rows, low_ok, 1.0))

    def pairs_of(layer, part=None):
        r0, row_groups = ((0, ext_rows // 2), (2, ext_rows // 2 - 2), (2, ext_rows // 2 - 2), (WIDE, rows // 2))[layer]
        margin = WIDE + 2 * (layer + 1)
        inner = [margin <= r0 + 2 * k < ext_rows - margin for k in range(row_groups)]
        mains = [(r0 + 2 * k, False) for k in range(row_groups) if part is None or inner[k] == (part == 0)]
        edges = [(2 * k, True) for k in range(per // 2)] if part != 0 else []
        return [items[k : k + 2] for items in (mains, edges) for k in range(0, len(items), 2)]

    def compute(layer, at, pair):
        last = layer == 3
        dst, sdst = (levels[0], strips[0]) if last else (levels[layer + 1], strips[layer + 1])
        columns = [
            jnp.concatenate([(strips if strip else levels)[layer][at + 1 + xi, r : r + 4].reshape(64, 128) for xi in range(4)], 0)
            for r, strip in pair
        ]
        wide = jnp.concatenate(columns, 1) if len(columns) > 1 else columns[0]
        got = jnp.dot(t_ref[layer, :192], wide, preferred_element_type=F32)
        for k, (r, strip) in enumerate(pair):
            part = got[:, 128 * k : 128 * (k + 1)]
            a = part[64:128] + pltpu.roll(part[:64], 1, 1) * not_first
            a = a + pltpu.roll(part[128:], 127, 1) * not_last
            a = a + bias_ref[layer]
            a = jnp.maximum(a, 0.2 * a)
            for xo in range(2):
                place = at + xo
                if isinstance(place, int) and place < 0:
                    continue
                for yo in range(2):
                    one = a[(2 * xo + yo) * 16 : (2 * xo + yo + 1) * 16]
                    if not last:
                        if strip:
                            one = one * strip_ok(r + yo)
                        elif r + yo < WIDE:
                            one = one * top_ok
                        elif r + yo >= WIDE + rows:
                            one = one * low_ok
                        if two_sided:
                            outside = ((place < WIDE) & (gx == 0)) | (
                                (place >= WIDE + depth) & (gx == counts["gx"] - 1)
                            )
                            one = one * jnp.where(outside, 0.0, 1.0)
                    one = one.astype(BF)
                    if strip:
                        sdst[place + 2, r + yo + 1] = one
                        if r + yo == 0:
                            sdst[place + 2, per + 1] = pltpu.roll(one, 128 - SEG, 1)
                        if r + yo == per - 1:
                            sdst[place + 2, 0] = pltpu.roll(one, SEG, 1)
                    else:
                        dst[place + 2, r + yo + 1] = one

    def group(layer, at, part=None):
        for pair in pairs_of(layer, part):
            yield pair[0][1]
            compute(layer, at, pair)

    def wave(k, during):
        events = [(0, "fill", None), (1, "fill", None)]
        for layer in range(4):
            main = [p for p in pairs_of(layer) if not p[0][1]]
            edge = [p for p in pairs_of(layer) if p[0][1]]
            at = 2 * k - 1 - layer
            events += [(i + LAG * layer, "pair", (layer, at, p)) for i, p in enumerate(main)]
            events += [(5 + len(edge) * i_ + 2 * layer * len(edge), "pair", (layer, at, p)) for i_, p in enumerate(edge)]
        late = [emit(*one) for one in during]
        for work in late:
            events += [(len(pairs_of(1)) + LAG + i, "emit", work) for i in range(6)]
        done = object()
        for _, kind, what in sorted(events, key=lambda e: e[0]):
            if kind == "fill":
                for _ in range(8):
                    next(strips_work, None)
            elif kind == "pair":
                if what[2][0][1]:
                    for _ in strips_work:
                        pass
                compute(*what)
            else:
                next(what, done)
        for work in late:
            for _ in work:
                pass

    def emit(part, half):
        turn = transposer()
        edge_turn = jnp.where(right, 0, 2 * WIDE)
        edge_ahead = jnp.where(right, WIDE, 0)
        edge_mask = lane_mask(lambda lane: ((lane + edge_ahead) & 127) < WIDE)
        inner_mask = lane_mask(lambda lane: ((lane + edge_ahead) & 127) >= WIDE)
        v, s = (levels[2], strips[2]) if part == 0 else (levels[0], strips[0])
        out_ref = halves[half_ids.index(half)]
        role = jnp.where(section == part, 0, 1)
        size = out_ref.shape[2]
        for i in range(size):
            p = own_at + half * size + i
            to = flip(i, size)
            starts = list(range(0, rows, 16))
            for k in range(0, len(starts), 2):
                some = starts[k : k + 2]
                blocks = []
                for y0 in some:
                    tiles = []
                    for y in range(y0, y0 + 16):
                        r = y + WIDE
                        j, yo = r // per, r % per
                        by = (128 - 3 * WIDE - SEG * j) % 128
                        edge = pltpu.roll(s[p + 2, yo + 1], by + edge_turn, 1)
                        tiles.append(v[p + 2, r + 1] * inner_mask + edge * edge_mask)
                    blocks.append(jnp.concatenate(tiles, 0))
                    yield
                for y0, block in zip(some, swap_rows(turn, blocks)):
                    out_ref[role, :, to, y0 : y0 + 16] = block

    def run(*works):
        works = list(works)
        while works:
            for work in list(works):
                at = next(work, "end")
                if at == "end":
                    works.remove(work)
                elif at is True:
                    for _ in strips_work:
                        pass

    filling = [fill(*one) for one in fills]
    for work in filling:
        next(work, None)
    strips_work = itertools.chain(*filling)
    for step in steps:
        if step[0] == "wave":
            wave(*step[1:])
        elif step[0] == "loop":
            run(strips_work)
            _, layer, x0, n = step

            def body(g, carry):
                run(group(layer, x0 + 2 * g))
                return carry

            lax.fori_loop(0, n, body, 0)
        else:
            works = [strips_work] if step[0] == "first" else []
            for one in step[1:]:
                works.append(emit(*one[1:]) if one[0] == "emit" else group(*one[1:]))
            run(*works)
    run(strips_work)


def place_kernel(two_sided, moves, *refs):
    sources, out_ref, sems = refs[-2 - len(moves) : -2], refs[-2], refs[-1]
    section = lax.axis_index("segment")
    flipped = False if two_sided else lax.axis_index("gx") == 1
    copies = []
    for k, (own, half) in enumerate(moves):
        source = sources[k].at[0] if own else sources[k]
        size = source.shape[1]
        start = half * size if two_sided else jnp.where(flipped, 1 - half, half) * size
        place = out_ref.at[section if own else 1 - section, :, pl.ds(start, size)]
        copies.append(pltpu.make_async_copy(source, place, sems.at[k]))
    for copy in copies:
        copy.start()
    for copy in copies:
        copy.wait()


VMEM = pl.BlockSpec(memory_space=pltpu.VMEM)
ANY = pl.BlockSpec(memory_space=pl.ANY)


def shards(counts, features, weights, biases):
    gx, gy, gz = (counts[a] for a in ("gx", "gy", "gz"))
    two_sided = gx != 2
    micro, chans, depth, rows, lanes = features.shape
    edge = jax.ShapeDtypeStruct((depth, WIDE, chans, lanes), BF)
    hbm = pl.BlockSpec(memory_space=pltpu.HBM)
    in_hbm = lambda v: pltpu.with_memory_space_constraint(v, pltpu.HBM)
    tiles, edge_z, edge_a, edge_b, table = pl.pallas_call(
        functools.partial(pack_kernel, not two_sided),
        out_shape=(
            jax.ShapeDtypeStruct((depth, rows, chans, lanes), BF),
            jax.ShapeDtypeStruct((depth, chans, lanes), BF),
            edge,
            edge,
            jax.ShapeDtypeStruct((2, 208, 256), BF),
        ),
        in_specs=[hbm] * 3,
        out_specs=(VMEM,) * 5,
        scratch_shapes=[
            pltpu.VMEM((chans, depth, rows, lanes), BF),
            pltpu.VMEM((2, 3, 3, 3, chans, chans), BF),
            pltpu.VMEM((2, chans), BF),
            pltpu.SemaphoreType.DMA((chans + 2,)),
        ],
        name="pack",
        compiler_params=pltpu.CompilerParams(vmem_limit_bytes=4 << 20),
        cost_estimate=pl.CostEstimate(flops=4_000_000, bytes_accessed=1_000_000, transcendentals=0),
    )(in_hbm(features), in_hbm(jnp.transpose(weights[0], (0, 3, 4, 5, 1, 2))), in_hbm(biases[0]))

    def along_x(low, high):
        if not two_sided:
            return [lax.ppermute(low, "gx", swap_pairs(2))]
        up = [(i, i + 1) for i in range(gx - 1)]
        return [lax.ppermute(high, "gx", up), lax.ppermute(low, "gx", [(j, i) for i, j in up])]

    raws = along_x(tiles, tiles)
    from_z = lax.ppermute(edge_z, "gz", swap_pairs(gz))
    at_z = from_z[:, None]
    from_b = lax.ppermute(
        jnp.concatenate([edge_b, at_z], 1), "gy", shifted_pairs(gy)
    )
    from_a = lax.ppermute(jnp.concatenate([edge_a, at_z], 1), "gy", swap_pairs(gy))
    halo = jnp.concatenate([from_a, from_b, at_z], 1)
    half = depth // 2
    if two_sided:
        halos = along_x(halo, halo)
    else:
        start = jnp.where(lax.axis_index("gx") == 0, half, 0)
        near_halo = along_x(lax.dynamic_slice_in_dim(halo, start, half, 0), None)
        far_halo = along_x(lax.dynamic_slice_in_dim(halo, half - start, half, 0), None)

    other = lax.ppermute(table, "segment", swap_pairs(2))
    ext = depth + (2 * WIDE if two_sided else WIDE)
    ext_rows = rows + 2 * WIDE
    per = -(-ext_rows * SEG // 128)
    per += per % 2
    state = [jax.ShapeDtypeStruct((ext + 2, ext_rows + 2, chans, lanes), BF)] * 4
    state += [jax.ShapeDtypeStruct((ext + 2, per + 2, chans, lanes), BF)] * 4
    half_shape = jax.ShapeDtypeStruct((2, chans, half, rows, lanes), BF)
    keep_shape = jax.ShapeDtypeStruct((micro, chans, depth, rows, lanes), BF)

    def stage(plan, blocks, edges, pair, before=(), aliases=(), half_ids=()):
        n = len(blocks)
        start = n + len(edges) + 2
        shapes = list(state)
        if not before:
            shapes += [jax.ShapeDtypeStruct((4, 208, 256), BF), jax.ShapeDtypeStruct((4, 64, 128), F32)]
        shapes += [half_shape] * len(half_ids)
        return pl.pallas_call(
            functools.partial(layer_kernel, two_sided, counts, (*plan, depth), n, len(edges), len(before), half_ids),
            out_shape=shapes,
            in_specs=[VMEM] * (start + len(before)),
            out_specs=[VMEM] * len(shapes),
            input_output_aliases={start + i: o for i, o in aliases},
            compiler_params=pltpu.CompilerParams(vmem_limit_bytes=24 << 20),
            cost_estimate=pl.CostEstimate(flops=2_000_000_000, bytes_accessed=4_000_000, transcendentals=0),
        )(*blocks, *edges, *pair, *before)

    def place(whole, sources, moves):
        return pl.pallas_call(
            functools.partial(place_kernel, two_sided, moves),
            out_shape=keep_shape,
            in_specs=[ANY] * len(whole) + [VMEM] * len(sources),
            out_specs=ANY,
            scratch_shapes=[pltpu.SemaphoreType.DMA((len(sources),))],
            input_output_aliases={0: 0} if whole else {},
            name="place",
            compiler_params=pltpu.CompilerParams(vmem_limit_bytes=2 << 20),
            cost_estimate=pl.CostEstimate(flops=0, bytes_accessed=500_000, transcendentals=0),
        )(*whole, *sources)

    def chain(k, part=None):
        return [("run", ("one", layer, 2 * k - 1 - layer, part)) for layer in range(4) if 2 * k - layer >= 0]

    def with_strips(steps):
        return [("first", *steps[0][1:])] + steps[1:]

    if two_sided:
        fills = [(p, 1, depth - WIDE + p, depth - WIDE + p) for p in range(WIDE)]
        fills += [(WIDE + p, 0, p, p) for p in range(depth)]
        fills += [(WIDE + depth + p, 2, p, p) for p in range(WIDE)]
        steps = []
        for layer in range(4):
            steps.append(("loop", layer, layer + 1, (ext - 2 * layer - 2) // 2))
            if layer % 2:
                steps += [("run", ("emit", layer // 2, 0)), ("run", ("emit", layer // 2, 1))]
        *_, first, second = stage((fills, steps), [tiles, *raws], [halo, *halos], (table, other), half_ids=(0, 1))
    else:
        same = [(k, k) for k in range(8)]
        fills = [(p, 0, p, None) for p in range(depth)]
        steps = chain(0, 0) + chain(1, 0)
        *state_now, t, bias = stage((fills, steps), [tiles], [], (table, other))
        fills = [(p, 0, None, p) for p in range(depth)]
        one, two, three = chain(1, 1)
        steps = with_strips(chain(0, 1)) + [one, two, (*three, ("emit", 0, 0))]
        *state_now, first = stage((fills, steps), [], [halo], (t, bias), state_now, same, (0,))
        fills = [(depth + p, 0, p, p) for p in range(half)]
        steps = [("wave", 2, [(0, 1)]), ("run", ("emit", 1, 0))]
        *state_now, first, second = stage(
            (fills, steps), raws, near_halo, (t, bias), [*state_now, first], same + [(8, 8)], (0, 1)
        )
        fills = [(depth + p, 0, p, p - half) for p in range(half, WIDE)]
        steps = [("wave", 3, []), ("run", ("emit", 1, 1))]
        *_, second = stage((fills, steps), raws, far_halo, (t, bias), [*state_now, second], same + [(8, 8)], (1,))

    got_first = lax.ppermute(first[1], "segment", swap_pairs(2))
    got_second = lax.ppermute(second[1], "segment", swap_pairs(2))
    whole = place([], [first, second, got_first], ((True, 0), (True, 1), (False, 0)))
    return place([whole], [got_second], ((False, 1),))[None]


def solution(mesh):
    placed = (
        P(None, None, "gx", "gy", "gz"),
        P("segment", None, None, None, None, None, None),
        P("segment", None, None),
    )

    def step(*args):
        return shards(dict(mesh.shape), *args)

    return jax.shard_map(
        step,
        mesh=mesh,
        in_specs=placed,
        out_specs=P("segment", None, None, "gx", "gy", "gz"),
        check_vma=False,
    )
```
